256 devices in a mesh: bag: 64 (over y, z, core), seq: 4 (over x).
Axes of the slice: x: 4, y: 4, z: 8, core: 2. Of those that a mesh axis runs over, the one named last changes fastest.
Arguments:
- video: bfloat16 [32768, 5120], P('bag'), may hold values from -6 to 6
- w_query: bfloat16 [5120, 5120], P('bag', 'seq'), may hold values from -0.078125 to 0.078125
- cond_kv: bfloat16 [64, 512, 2, 5120], P('bag', None, None, 'seq'), may hold values from -400 to 400, as said below
- neg_kv: bfloat16 [512, 2, 5120], P('bag', None, 'seq'), may hold values from -400 to 400, as said below
- prompt_len: int32 [64], P('bag'), may hold values from 1 to 512
- neg_len: int32 [1], replicated, may hold values from 1 to 512
Outputs:
- guided: bfloat16 [32768, 5120], P('bag', 'seq')
The draws below stay inside these ranges and needn't reach their ends.
Inputs may be any that keep to these rules, and one draw needn't show every extreme that they name: `cond_kv`: finite keys and values. `neg_kv`: finite keys and values.
All inputs are finite; a program needn't handle non-finite values.
Results may differ from the reference program's by a relative error of at most 0.012.
The reference program's roundings to bfloat16 on the way count: a program that leaves them out, or rounds other values in their place, can miss the bound.
Values may be sent and summed in bfloat16 or wider, within the bound.
No kernel may reach another device: no remote copies, remote signals or barrier semaphores. Data moves between devices by JAX's collectives and lax.ppermute only.
A program may use at most 128 MiB of HBM per device.

```python
import jax
import jax.numpy as jnp
from jax import lax

DM = 5120
HEADS = 40
HD = 128
PLEN = 512
TOK_DEV = 512
BAGS = 64
TOKENS = 32768


def kv_rows(key, count):
    keys_list = jax.random.split(key, 2)
    base = jax.random.normal(keys_list[0], (count, PLEN, DM), jnp.float32)
    values = jax.random.normal(keys_list[1], (count, PLEN, DM), jnp.float32)
    keys = base
    return jnp.stack([keys, values], axis=2)


def draw_cond_kv(key, part):
    return kv_rows(jax.random.fold_in(key, 11), BAGS).astype(jnp.bfloat16)


def draw_neg_kv(key, part):
    return kv_rows(jax.random.fold_in(key, 23), 1)[0].astype(jnp.bfloat16)


def place_ends(drawn, own_key, least, high):
    spot = [jax.random.randint(jax.random.fold_in(own_key, axis), (), 0, length) for axis, length in enumerate(drawn.shape)]
    longest = drawn.shape.index(max(drawn.shape))
    next_to = spot[:longest] + [(spot[longest] + 1) % drawn.shape[longest]] + spot[longest + 1:]
    return drawn.at[tuple(spot)].set(least).at[tuple(next_to)].set(high)


def shard_levels(key, dims, cuts, smallest, high):
    def one(axis_at, blocks):
        draws = jax.random.uniform(jax.random.fold_in(jax.random.fold_in(key, 6), axis_at), (blocks,), jnp.float32, smallest / len(cuts), high / len(cuts))
        return jnp.repeat(jnp.exp(draws), dims[axis_at] // blocks).reshape((-1,) + (1,) * (len(dims) - axis_at - 1))

    level = one(*cuts[0])
    for cut in cuts[1:]:
        level = level * one(*cut)
    return level


def scatter_about(stream_key, dims, scale, limit, cuts=(), kind=jnp.bfloat16):
    level = shard_levels(stream_key, dims, cuts, -0.22, 0.18) if cuts else 1.0
    drawn = jax.random.normal(stream_key, dims, jnp.float32) * scale * level
    return jnp.minimum(jnp.maximum(drawn, -limit), limit).astype(kind)


def setup_inputs(seed: int = 0) -> dict:
    streams_of = jax.random.split(jax.random.key(seed), 7)
    return {
        "video": scatter_about(streams_of[0], (TOKENS, DM), 1.0, 6.0, ((0, 64),)),
        "w_query": scatter_about(streams_of[1], (DM, DM), DM ** -0.5, 0.078125, ((0, 64), (1, 4))),
        "cond_kv": draw_cond_kv(jax.random.fold_in(streams_of[6], 71), 0),
        "neg_kv": draw_neg_kv(jax.random.fold_in(streams_of[6], 71), 0),
        "prompt_len": place_ends(jax.random.randint(streams_of[4], (BAGS,), 1, PLEN + 1), jax.random.fold_in(streams_of[4], 1), 1, PLEN).astype(jnp.int32),
        "neg_len": jax.random.randint(streams_of[5], (1,), 1, PLEN + 1).astype(jnp.int32),
    }


guidance_scale = 5.0

def layer_norm(video):
    values = video.astype(jnp.float32)
    center = values - lax.optimization_barrier(jnp.mean(values, axis=-1, keepdims=True))
    spread = lax.optimization_barrier(jnp.mean(center * center, axis=-1, keepdims=True))
    return (center * lax.rsqrt(spread + 1e-06)).astype(jnp.bfloat16)

def attend(query_rms, keys, values, length):
    tok_rows = query_rms.shape[0]
    q_heads = query_rms.reshape(tok_rows, HEADS, HD).astype(jnp.float32)
    k_heads = keys.reshape(PLEN, HEADS, HD).astype(jnp.float32)
    v_heads = values.reshape(PLEN, HEADS, HD).astype(jnp.float32)
    scores = jnp.einsum('thd,shd->hts', q_heads, k_heads) / jnp.sqrt(jnp.float32(HD))
    live = (jnp.arange(PLEN, dtype=jnp.int32) < length)[None, None, :]
    scores = jnp.where(live, scores, jnp.float32(-1e+30))
    top = lax.optimization_barrier(jnp.max(scores, axis=-1, keepdims=True))
    weights = jnp.where(live, jnp.exp(scores - top), jnp.float32(0.0))
    weights = (weights / lax.optimization_barrier(jnp.sum(weights, axis=-1, keepdims=True))).astype(jnp.bfloat16)
    mixed = jnp.einsum('hts,shd->thd', weights.astype(jnp.float32), v_heads)
    return mixed.reshape(tok_rows, HEADS * HD)

def reference(video, w_query, cond_kv, neg_kv, prompt_len, neg_len):
    per_bag = video.reshape(BAGS, TOK_DEV, DM)

    def one_bag(items):
        tokens, table, length = items
        normed = layer_norm(tokens)
        query = jnp.dot(normed, w_query, preferred_element_type=jnp.float32)
        query_rms = (query * lax.rsqrt(lax.optimization_barrier(jnp.mean(query * query, axis=-1, keepdims=True)) + 1e-06)).astype(jnp.bfloat16)
        cond = attend(query_rms, table[:, 0], table[:, 1], length)
        uncond = attend(query_rms, neg_kv[:, 0], neg_kv[:, 1], neg_len[0])
        return (uncond + guidance_scale * (cond - uncond)).astype(jnp.bfloat16)
    guided = lax.map(one_bag, (per_bag, cond_kv, prompt_len))
    return guided.reshape(BAGS * TOK_DEV, DM)
```

```python
import jax
import jax.numpy as jnp
from jax import lax
from jax.experimental import pallas as pl
from jax.experimental.pallas import tpu as pltpu
from jax.sharding import Mesh, PartitionSpec as P

DM = 5120
HD = 128
TOK = 512
PLEN = 512
NY, NZ, NC, NX = 4, 8, 2, 4
COLS = DM // NX
NA = 640
NB = COLS - NA
ROWS = DM // (NY * NZ * NC)
NEGS = PLEN // (NY * NZ * NC)
WR = NC * ROWS
BR = NC * (ROWS + 2 * NEGS)
GUIDE = 5.0
VMEM_LIMIT = 60 * 1024 * 1024


def swap_cores(a):
    return lax.ppermute(a, "c", [(0, 1), (1, 0)])


def shift(a, axis, n):
    pairs = [(2 * i, 2 * ((i + 1) % n)) for i in range(n)]
    pairs += [(2 * i + 1, 2 * ((i - 1) % n) + 1) for i in range(n)]
    return lax.ppermute(a, (axis, "c"), pairs)


def half(a, which):
    r, n = a.shape
    return lax.dynamic_index_in_dim(a.reshape(2, r // 2, n), which, 0, keepdims=False)


def ring(own, axis, n, me, d, c):
    got = []
    cur = own
    for _ in range(n // 2 - 1):
        cur = shift(cur, axis, n)
        got.append(cur)
    got.append(shift(half(cur, c), axis, n))
    return got


def place(own, got, other, n, me, d, c):
    r, cols = own.shape
    buf = jnp.zeros((2 * n, r // 2, cols), own.dtype)

    def put(buf, a, at):
        return lax.dynamic_update_slice(buf, a.reshape(-1, r // 2, cols), (at, 0, 0))

    buf = put(buf, own, 2 * me)
    for k in range(1, n // 2):
        buf = put(buf, got[k - 1], 2 * lax.rem(me - k * d + n, n))
        buf = put(buf, other[k - 1], 2 * lax.rem(me + k * d + n, n))
    far = 2 * lax.rem(me + n // 2, n)
    buf = put(buf, got[-1], far + c)
    buf = put(buf, other[-1], far + 1 - c)
    return buf.reshape(n * r, cols)


def norm_kernel(v_ref, la_ref, lb_ref):
    v = v_ref[...].astype(jnp.float32)
    center = v - jnp.mean(v, axis=-1, keepdims=True)
    spread = jnp.mean(center * center, axis=-1, keepdims=True)
    out = center * lax.rsqrt(spread + 1e-06)
    for y in range(NY):
        lb_ref[y] = out[:, y * NZ * WR:(y + 1) * NZ * WR].astype(jnp.bfloat16)
    for z in range(NZ):
        parts = [out[:, (y * NZ + z) * WR:(y * NZ + z + 1) * WR] for y in range(NY)]
        la_ref[z] = jnp.concatenate(parts, axis=1).astype(jnp.bfloat16)


def layer_norm(video):
    tm = 64
    return pl.pallas_call(
        norm_kernel,
        grid=(TOK // tm,),
        in_specs=[pl.BlockSpec((tm, DM), lambda i: (i, 0))],
        out_specs=[
            pl.BlockSpec((NZ, tm, NY * WR), lambda i: (0, i, 0)),
            pl.BlockSpec((NY, tm, NZ * WR), lambda i: (0, i, 0)),
        ],
        out_shape=[
            jax.ShapeDtypeStruct((NZ, TOK, NY * WR), jnp.bfloat16),
            jax.ShapeDtypeStruct((NY, TOK, NZ * WR), jnp.bfloat16),
        ],
        compiler_params=pltpu.CompilerParams(vmem_limit_bytes=VMEM_LIMIT),
        cost_estimate=pl.CostEstimate(flops=30_000_000, bytes_accessed=15_000_000, transcendentals=0),
        name="norm",
    )(video)


def project_kernel(za_ref, yb_ref, la_ref, lb_ref, *refs):
    q_ref = refs[-1]
    a_refs, b_refs = refs[:NZ], refs[NZ:NZ + NY]
    for (n, ref_list, l_ref, at, lo) in (
        (NY, a_refs, la_ref, za_ref, 0), (NZ, b_refs, lb_ref, yb_ref, NA)
    ):
        for t in range(0, TOK, 256):
            total = None
            for k, w_ref in enumerate(ref_list):
                w = w_ref[...].reshape(n, BR, w_ref.shape[-1])[:, :WR]
                w = w.reshape(n * WR, w_ref.shape[-1])
                left = l_ref[at[k], t:t + 256]
                part = jnp.dot(left, w, preferred_element_type=jnp.float32)
                total = part if total is None else total + part
            q_ref[t:t + 256, lo:lo + total.shape[1]] = total


def project(za, yb, la, lb, a_list, b_list):
    vm = pl.BlockSpec(memory_space=pltpu.VMEM)
    sm = pl.BlockSpec(memory_space=pltpu.SMEM)
    return pl.pallas_call(
        project_kernel,
        in_specs=[sm, sm] + [vm] * (2 + len(a_list) + len(b_list)),
        out_specs=vm,
        out_shape=jax.ShapeDtypeStruct((TOK, COLS), jnp.float32),
        compiler_params=pltpu.CompilerParams(vmem_limit_bytes=VMEM_LIMIT),
        cost_estimate=pl.CostEstimate(flops=2 * TOK * DM * COLS, bytes_accessed=29_000_000, transcendentals=0),
        name="project",
    )(za, yb, la, lb, *a_list, *b_list)


def attend_kernel(len_ref, q_ref, r_ref, ck_ref, cv_ref, nk_ref, nv_ref, o_ref):
    q = (q_ref[...] * r_ref[...]).astype(jnp.bfloat16)
    slot = lax.broadcasted_iota(jnp.int32, (1, PLEN), 1)
    scale = 1.0 / (HD ** 0.5)

    def one(k_ref, v_ref, length):
        bias = jnp.where(slot < length, 0.0, -1e30).astype(jnp.float32)
        s = lax.dot_general(q, k_ref[...], (((1,), (1,)), ((), ())), preferred_element_type=jnp.float32)
        s = s * scale + bias
        e = jnp.exp(s - jnp.max(s, axis=-1, keepdims=True))
        w = (e * (1.0 / jnp.sum(e, axis=-1, keepdims=True))).astype(jnp.bfloat16)
        return jnp.dot(w, v_ref[...], preferred_element_type=jnp.float32)

    cond = one(ck_ref, cv_ref, len_ref[0])
    uncond = one(nk_ref, nv_ref, len_ref[1])
    o_ref[...] = (uncond + GUIDE * (cond - uncond)).astype(jnp.bfloat16)


def attend(lens, q, r, ck, cv, nk, nv):
    col = pl.BlockSpec((TOK, HD), lambda h: (0, h))
    return pl.pallas_call(
        attend_kernel,
        grid=(COLS // HD,),
        in_specs=[
            pl.BlockSpec(memory_space=pltpu.SMEM),
            col,
            pl.BlockSpec((TOK, 1), lambda h: (0, 0)),
            col, col, col, col,
        ],
        out_specs=col,
        out_shape=jax.ShapeDtypeStruct((TOK, COLS), jnp.bfloat16),
        compiler_params=pltpu.CompilerParams(vmem_limit_bytes=VMEM_LIMIT),
        cost_estimate=pl.CostEstimate(flops=8 * TOK * PLEN * COLS, bytes_accessed=10_000_000, transcendentals=2 * TOK * PLEN * 10),
        name="attend",
    )(lens, q, r, ck, cv, nk, nv)


def body(video, w_query, cond_kv, neg_kv, prompt_len, neg_len):
    y, z, c = lax.axis_index("y"), lax.axis_index("z"), lax.axis_index("c")
    d = 1 - 2 * c

    neg = neg_kv.transpose(1, 0, 2).reshape(2 * NEGS, COLS)
    own = jnp.concatenate([w_query, neg], axis=0)
    oth = swap_cores(own)
    first = jnp.where(c == 0, own, oth)
    second = jnp.where(c == 0, oth, own)
    block = jnp.concatenate([first[:ROWS], second[:ROWS], first[ROWS:], second[ROWS:]], axis=0)
    a0, b0 = block[:, :NA], block[:, NA:]

    def finish(got):
        sizes = [g.shape[0] for g in got]
        both = swap_cores(jnp.concatenate(got, axis=0))
        out, at = [], 0
        for s in sizes:
            out.append(both[at:at + s])
            at += s
        return out

    ay = ring(a0, "y", NY, y, d, c)
    bz = ring(b0, "z", NZ, z, d, c)
    a1 = place(a0, ay, finish(ay), NY, y, d, c)
    b1 = place(b0, bz, finish(bz), NZ, z, d, c)
    az = ring(a1, "z", NZ, z, d, c)
    by = ring(b1, "y", NY, y, d, c)
    azo = [swap_cores(g) for g in az]
    byo = [swap_cores(g) for g in by]

    def join(mine, theirs):
        r, n = mine.shape
        buf = jnp.zeros((2, r, n), mine.dtype)
        buf = lax.dynamic_update_slice(buf, mine[None], (c, 0, 0))
        buf = lax.dynamic_update_slice(buf, theirs[None], (1 - c, 0, 0))
        return buf.reshape(2 * r, n)

    a_list, za = [a1], [z]
    for k in range(1, NZ // 2):
        a_list += [az[k - 1], azo[k - 1]]
        za += [z - k * d, z + k * d]
    a_list.append(join(az[-1], azo[-1]))
    za.append(z + NZ // 2)
    b_list, yb = [b1], [y]
    for k in range(1, NY // 2):
        b_list += [by[k - 1], byo[k - 1]]
        yb += [y - k * d, y + k * d]
    b_list.append(join(by[-1], byo[-1]))
    yb.append(y + NY // 2)
    za = lax.rem(jnp.stack(za) + NZ, NZ).astype(jnp.int32)
    yb = lax.rem(jnp.stack(yb) + NY, NY).astype(jnp.int32)

    la, lb = layer_norm(video)
    q = project(za, yb, la, lb, a_list, b_list)
    squares = lax.psum(jnp.sum(q * q, axis=1), "x")
    r = lax.rsqrt(squares / DM + 1e-06)[:, None]

    def negative(chunks, n, at):
        tail = [g.reshape(n, BR, g.shape[-1])[:, WR:] for g in chunks]
        order = jnp.zeros((len(chunks), n) + tail[0].shape[1:], tail[0].dtype)
        for k, g in enumerate(tail):
            order = lax.dynamic_update_slice(order, g[None], (at[k], 0, 0, 0))
        return order.reshape(len(chunks), n, NC, 2, NEGS, -1)

    na = negative(a_list, NY, za).transpose(3, 1, 0, 2, 4, 5).reshape(2, PLEN, NA)
    nb = negative(b_list, NZ, yb).transpose(3, 0, 1, 2, 4, 5).reshape(2, PLEN, NB)
    nk = jnp.concatenate([na[0], nb[0]], axis=1)
    nv = jnp.concatenate([na[1], nb[1]], axis=1)
    ck, cv = cond_kv[0, :, 0], cond_kv[0, :, 1]
    lens = jnp.concatenate([prompt_len, neg_len])
    return attend(lens, q, r, ck, cv, nk, nv)


def solution(mesh):
    mesh4 = Mesh(mesh.devices.reshape(NY, NZ, NC, NX), ("y", "z", "c", "x"))
    bag = ("y", "z", "c")
    in_specs = (
        P(bag, None),
        P(bag, "x"),
        P(bag, None, None, "x"),
        P(bag, None, "x"),
        P(bag),
        P(),
    )
    return jax.shard_map(body, mesh=mesh4, in_specs=in_specs, out_specs=P(bag, "x"), check_vma=False)
```

```python
import functools
import math

import jax
import jax.numpy as jnp
from jax import lax
from jax.experimental import pallas as pl
from jax.experimental.pallas import tpu as pltpu
from jax.sharding import Mesh, PartitionSpec as P

DM = 5120
HD = 128
TOK = 512
PARTS = 4
TH = TOK // PARTS
PLEN = 512
NY, NZ, NC, NX = 4, 8, 2, 4
COLS = DM // NX
NA = 640
NB = COLS - NA
ROWS = DM // (NY * NZ * NC)
NEGS = PLEN // (NY * NZ * NC)
WR = NC * ROWS
BR = NC * (ROWS + 2 * NEGS)
GUIDE = 5.0
VMEM_LIMIT = 60 * 1024 * 1024


def swap_cores(a, tag):
    with jax.named_scope(tag):
        return lax.ppermute(a, "c", [(0, 1), (1, 0)])


def shift(a, axis, n, tag, by=1):
    pairs = [(2 * i, 2 * ((i + by) % n)) for i in range(n)]
    pairs += [(2 * i + 1, 2 * ((i - by) % n) + 1) for i in range(n)]
    with jax.named_scope(tag):
        return lax.ppermute(a, (axis, "c"), pairs)


def together(*arrays):
    return lax.optimization_barrier(arrays)


def half(a, which):
    r, n = a.shape
    return lax.dynamic_index_in_dim(a.reshape(2, r // 2, n), which, 0, keepdims=False)


def place(own, got, other, n, me, d, c):
    r, cols = own.shape
    buf = jnp.zeros((2 * n, r // 2, cols), own.dtype)

    def put(buf, a, at):
        return lax.dynamic_update_slice(buf, a.reshape(-1, r // 2, cols), (at, 0, 0))

    buf = put(buf, own, 2 * me)
    for k in range(1, n // 2):
        buf = put(buf, got[k - 1], 2 * lax.rem(me - k * d + n, n))
        buf = put(buf, other[k - 1], 2 * lax.rem(me + k * d + n, n))
    far = 2 * lax.rem(me + n // 2, n)
    buf = put(buf, got[-1], far + c)
    buf = put(buf, other[-1], far + 1 - c)
    return buf.reshape(n * r, cols)


def norm_kernel(v_ref, la_ref, lb_ref):
    def step(i, _):
        rows = pl.ds(pl.multiple_of(i * 16, 16), 16)
        v = v_ref[rows, :].astype(jnp.float32)
        center = v - jnp.mean(v, axis=-1, keepdims=True)
        spread = jnp.mean(center * center, axis=-1, keepdims=True)
        out = center * lax.rsqrt(spread + 1e-06)
        for y in range(NY):
            lb_ref[y, rows, :] = out[:, y * NZ * WR:(y + 1) * NZ * WR].astype(jnp.bfloat16)
        for z in range(NZ):
            parts = [out[:, (y * NZ + z) * WR:(y * NZ + z + 1) * WR] for y in range(NY)]
            la_ref[z, rows, :] = jnp.concatenate(parts, axis=1).astype(jnp.bfloat16)
        return 0

    lax.fori_loop(0, v_ref.shape[0] // 16, step, 0)


def layer_norm(video, part):
    tm, steps = 64, TH // 64
    return pl.pallas_call(
        norm_kernel,
        grid=(steps,),
        in_specs=[pl.BlockSpec((tm, DM), lambda i: (part * steps + i, 0))],
        out_specs=[
            pl.BlockSpec((NZ, tm, NY * WR), lambda i: (0, i, 0)),
            pl.BlockSpec((NY, tm, NZ * WR), lambda i: (0, i, 0)),
        ],
        out_shape=[
            jax.ShapeDtypeStruct((NZ, TH, NY * WR), jnp.bfloat16),
            jax.ShapeDtypeStruct((NY, TH, NZ * WR), jnp.bfloat16),
        ],
        compiler_params=pltpu.CompilerParams(vmem_limit_bytes=32 * 1024 * 1024),
        cost_estimate=pl.CostEstimate(flops=15_000_000, bytes_accessed=8_000_000, transcendentals=0),
        name="norm",
    )(video)


def project_kernel(n, chunks, first, last, at_ref, *refs):
    l_refs, refs = refs[:PARTS], refs[PARTS:]
    q_ref = refs[-2] if last else refs[-1]
    at = 0
    rights = []
    for count in chunks:
        got = [r[...] for r in refs[at:at + count]]
        at += count
        if count == 2:
            even = at_ref[len(chunks)] == 0
            got = [jnp.where(even, got[0], got[1]), jnp.where(even, got[1], got[0])]
        per = n // count
        got = [w.reshape(per, BR, w.shape[-1])[:, :WR].reshape(per * WR, w.shape[-1]) for w in got]
        rights.append(got[0] if count == 1 else jnp.concatenate(got, axis=0))
    for h, l_ref in enumerate(l_refs):
        rows = slice(h * TH, (h + 1) * TH)
        total = None if first else refs[at][rows, :]
        for k, w in enumerate(rights):
            part = jnp.dot(l_ref[at_ref[k]], w, preferred_element_type=jnp.float32)
            total = part if total is None else total + part
        q_ref[rows, :] = total
        if last:
            square = total * total
            lanes = square[:, :128]
            for j in range(128, square.shape[1], 128):
                lanes = lanes + square[:, j:j + 128]
            refs[-1][:, rows] = jnp.sum(lanes.T, axis=0, keepdims=True)


def project(q, n, at, c, left, chunks, last=False):
    vm = pl.BlockSpec(memory_space=pltpu.VMEM)
    sm = pl.BlockSpec(memory_space=pltpu.SMEM)
    flat = [a for chunk in chunks for a in chunk]
    cols = flat[0].shape[-1]
    first = q is None
    at = jnp.stack([*at, c]).astype(jnp.int32)
    extra = [] if first else [q]
    q_shape = jax.ShapeDtypeStruct((TOK, cols), jnp.float32)
    return pl.pallas_call(
        functools.partial(project_kernel, n, [len(chunk) for chunk in chunks], first, last),
        in_specs=[sm] + [vm] * (PARTS + len(flat) + len(extra)),
        out_specs=[vm, vm] if last else vm,
        out_shape=[q_shape, jax.ShapeDtypeStruct((1, TOK), jnp.float32)] if last else q_shape,
        input_output_aliases={} if first else {1 + PARTS + len(flat): 0},
        compiler_params=pltpu.CompilerParams(vmem_limit_bytes=40 * 1024 * 1024),
        cost_estimate=pl.CostEstimate(
            flops=2 * TOK * n * WR * cols * len(chunks),
            bytes_accessed=len(chunks) * 2_000_000 + 2_600_000, transcendentals=0),
        name="project",
    )(at, *left, *flat, *extra)


def attend_kernel(len_ref, qa_ref, qb_ref, s0, s1, s2, s3, ck_ref, cv_ref, na_ref, nb_ref, o_ref, r_ref, one_ref, cm_ref, nm_ref):
    head = pl.program_id(0)

    @pl.when(head == 0)
    def _():
        squares = (s0[...] + s1[...]) + (s2[...] + s3[...])
        r = lax.rsqrt(squares * (1.0 / DM) + 1e-06)
        r_ref[...] = jnp.broadcast_to(r, (HD, TOK)).T
        lane = lax.broadcasted_iota(jnp.int32, (PLEN, HD), 1)
        slot = lax.broadcasted_iota(jnp.int32, (PLEN, HD), 0)
        one_ref[...] = jnp.where(lane == 0, 1.0, 0.0).astype(jnp.bfloat16)
        for m_ref, length in ((cm_ref, len_ref[0]), (nm_ref, len_ref[1])):
            dead = jnp.logical_and(lane == 0, slot >= length)
            m_ref[...] = jnp.where(dead, -1e30, 0.0).astype(jnp.bfloat16)

    in_a = head < NA // HD
    q = (jnp.where(in_a, qa_ref[...], qb_ref[...]) * r_ref[...]).astype(jnp.bfloat16)
    q = jnp.concatenate([q, one_ref[...]], axis=1)
    neg = jnp.where(in_a, na_ref[...], nb_ref[...])
    scale = math.log2(math.e) / math.sqrt(HD)

    def one(k, m, v):
        k = jnp.concatenate([k, m], axis=1)
        s = lax.dot_general(q, k, (((1,), (1,)), ((), ())), preferred_element_type=jnp.float32)
        e = jnp.exp2((s - jnp.max(s, axis=-1, keepdims=True)) * scale)
        w = (e * (1.0 / jnp.sum(e, axis=-1, keepdims=True))).astype(jnp.bfloat16)
        return jnp.dot(w, v, preferred_element_type=jnp.float32)

    cond = one(ck_ref[...], cm_ref[...], cv_ref[...])
    uncond = one(neg[0], nm_ref[...], neg[1])
    o_ref[...] = (uncond + GUIDE * (cond - uncond)).astype(jnp.bfloat16)


def attend(lens, qa, qb, squares, ck, cv, na, nb):
    col = pl.BlockSpec((TOK, HD), lambda h: (0, h))
    row = pl.BlockSpec((1, TOK), lambda h: (0, 0))
    last_a = NA // HD - 1
    in_a = lambda h: jnp.minimum(h, last_a)
    in_b = lambda h: jnp.maximum(h - last_a - 1, 0)
    return pl.pallas_call(
        attend_kernel,
        grid=(COLS // HD,),
        in_specs=[
            pl.BlockSpec(memory_space=pltpu.SMEM),
            pl.BlockSpec((TOK, HD), lambda h: (0, in_a(h))),
            pl.BlockSpec((TOK, HD), lambda h: (0, in_b(h))),
            row, row, row, row,
            col, col,
            pl.BlockSpec((2, PLEN, HD), lambda h: (0, 0, in_a(h))),
            pl.BlockSpec((2, PLEN, HD), lambda h: (0, 0, in_b(h))),
        ],
        out_specs=col,
        out_shape=jax.ShapeDtypeStruct((TOK, COLS), jnp.bfloat16),
        scratch_shapes=[pltpu.VMEM((TOK, HD), jnp.float32)] + [pltpu.VMEM((TOK, HD), jnp.bfloat16)] * 3,
        compiler_params=pltpu.CompilerParams(vmem_limit_bytes=32 * 1024 * 1024),
        cost_estimate=pl.CostEstimate(flops=8 * TOK * PLEN * COLS, bytes_accessed=10_000_000, transcendentals=2 * TOK * PLEN * 10),
        name="attend",
    )(lens, qa, qb, *squares, ck, cv, na, nb)


def body(video, w_query, cond_kv, neg_kv, prompt_len, neg_len):
    y, z, c = lax.axis_index("y"), lax.axis_index("z"), lax.axis_index("c")
    d = 1 - 2 * c

    neg = neg_kv.transpose(1, 0, 2).reshape(2 * NEGS, COLS)
    own = jnp.concatenate([w_query, neg], axis=0)
    oth = swap_cores(own, "s0")
    first = jnp.where(c == 0, own, oth)
    second = jnp.where(c == 0, oth, own)
    block = jnp.concatenate([first[:ROWS], second[:ROWS], first[ROWS:], second[ROWS:]], axis=0)
    a0, b0 = block[:, :NA], block[:, NA:]

    def norm(i, *deps):
        with jax.named_scope(f"norm{i}"):
            return layer_norm(together(video, *deps)[0] if deps else video, i)

    def finish(got, tag):
        both = swap_cores(jnp.concatenate(got, axis=0), tag)
        out, at = [], 0
        for g in got:
            out.append(both[at:at + g.shape[0]])
            at += g.shape[0]
        return out

    ay1 = shift(a0, "y", NY, "ay1")
    bz1 = shift(b0, "z", NZ, "bz1")
    bz2 = shift(b0, "z", NZ, "bz2", 2)
    n0 = norm(0)
    ay1, bz1, bz2, n0 = together(ay1, bz1, bz2, n0)

    ay2 = shift(half(ay1, c), "y", NY, "ay2")
    bz3 = shift(bz2, "z", NZ, "bz3")
    bz4 = shift(half(bz2, c), "z", NZ, "bz4", 2)
    n1 = norm(1, n0[0])
    ay2, n1 = together(ay2, n1)

    a1 = place(a0, [ay1, ay2], finish([ay1, ay2], "as"), NY, y, d, c)
    a1, cond_kv = together(a1, cond_kv)
    af0, ag0 = half(a1, c), half(a1, 1 - c)
    af1 = shift(af0, "z", NZ, "af1")
    n2 = norm(2, n1[0], a1)
    bz = [bz1, bz2, bz3, bz4]
    b1 = place(b0, bz, finish(bz, "bs"), NZ, z, d, c)
    n2, ag0, b1 = together(n2, ag0, b1)
    ag1 = shift(ag0, "z", NZ, "ag1")
    bf0, bg0 = half(b1, c), half(b1, 1 - c)
    bf1, bg1 = shift(bf0, "y", NY, "bf1"), shift(bg0, "y", NY, "bg1")
    n3 = norm(3, n2[0])
    af1, n3 = together(af1, n3)
    af2 = shift(af1, "z", NZ, "af2")
    ag2 = shift(ag1, "z", NZ, "ag2")
    af2, bf1 = together(af2, bf1)
    bf2 = shift(bf1, "y", NY, "bf2")
    af3 = shift(af2, "z", NZ, "af3")
    ag3 = shift(ag2, "z", NZ, "ag3")
    af4 = shift(af3, "z", NZ, "af4")
    az = [(af1, ag1), (af2, ag2), (af3, ag3), (af4,)]
    by = [(bf1, bg1), (bf2,)]
    norms = (n0, n1, n2, n3)
    la, lb = [m[0] for m in norms], [m[1] for m in norms]

    def other(hop, tag):
        return tuple(swap_cores(a, tag + t) for a, t in zip(hop, "fg"))

    azo = [other(h, f"as{k}") for k, h in enumerate(az, 1)]
    byo = [other(h, f"bs{k}") for k, h in enumerate(by, 1)]

    def at(me, k, n):
        return lax.rem(me + k * d + n, n)

    qa = project(None, NY, [z], c, la, [(a1,)])
    qb = project(None, NZ, [y], c, lb, [(b1,)])
    for k in range(1, NZ // 2):
        qa = project(qa, NY, [at(z, -k, NZ), at(z, k, NZ)], c, la, [az[k - 1], azo[k - 1][::-1]])
    qa, sa = project(qa, NY, [at(z, NZ // 2, NZ)], c, la, [(az[-1][0], azo[-1][0])], last=True)
    for k in range(1, NY // 2):
        qb = project(qb, NZ, [at(y, -k, NY), at(y, k, NY)], c, lb, [by[k - 1], byo[k - 1][::-1]])
    qb, sb = project(qb, NZ, [at(y, NY // 2, NY)], c, lb, [(by[-1][0], byo[-1][0])], last=True)
    part = sa + sb
    squares = [part] + [lax.ppermute(part, "x", [(i, (i + k) % NX) for i in range(NX)]) for k in (1, 2, 3)]

    def negative(own, hops, others, n, me):
        m = 2 * len(hops)
        cols = own.shape[-1]
        buf = jnp.zeros((m, 2, n // 2, BR - WR, cols), own.dtype)

        def put(buf, a, at, which):
            rows = a.reshape(-1, n // 2, BR, cols)[:, :, WR:]
            return lax.dynamic_update_slice(buf, rows[None], (at, which, 0, 0, 0))

        buf = put(buf, own, me, 0)
        for k in range(1, m // 2):
            for i, which in enumerate((c, 1 - c)):
                buf = put(buf, hops[k - 1][i], at(me, -k, m), which)
                buf = put(buf, others[k - 1][i], at(me, k, m), 1 - which)
        far = at(me, m // 2, m)
        buf = put(buf, hops[-1][0], far, c)
        buf = put(buf, others[-1][0], far, 1 - c)
        return buf.reshape(m, n, NC, 2, NEGS, cols)

    na = negative(a1, az, azo, NY, z).transpose(3, 1, 0, 2, 4, 5).reshape(2, PLEN, NA)
    nb = negative(b1, by, byo, NZ, y).transpose(3, 0, 1, 2, 4, 5).reshape(2, PLEN, NB)
    ck, cv = cond_kv[0, :, 0], cond_kv[0, :, 1]
    lens = jnp.concatenate([prompt_len, neg_len])
    return attend(lens, qa, qb, squares, ck, cv, na, nb)


def solution(mesh):
    mesh4 = Mesh(mesh.devices.reshape(NY, NZ, NC, NX), ("y", "z", "c", "x"))
    bag = ("y", "z", "c")
    in_specs = (
        P(bag, None),
        P(bag, "x"),
        P(bag, None, None, "x"),
        P(bag, None, "x"),
        P(bag),
        P(),
    )
    return jax.shard_map(body, mesh=mesh4, in_specs=in_specs, out_specs=P(bag, "x"), check_vma=False)
```

```python
import functools
import math

import jax
import jax.numpy as jnp
from jax import lax
from jax.experimental import pallas as pl
from jax.experimental.pallas import tpu as pltpu
from jax.sharding import Mesh, PartitionSpec as P

DM = 5120
HD = 128
TOK = 512
SPLIT = (0, 128, TOK)
PARTS = len(SPLIT) - 1
PLEN = 512
NY, NZ, NC, NX = 4, 8, 2, 4
COLS = DM // NX
NA = 640
NB = COLS - NA
ROWS = DM // (NY * NZ * NC)
NEGS = PLEN // (NY * NZ * NC)
WR = NC * ROWS
BR = NC * (ROWS + 2 * NEGS)
GUIDE = 5.0
VMEM_LIMIT = 60 * 1024 * 1024


def swap_cores(a, tag):
    with jax.named_scope(tag):
        return lax.ppermute(a, "c", [(0, 1), (1, 0)])


def shift(a, axis, n, tag, by=1):
    pairs = [(2 * i, 2 * ((i + by) % n)) for i in range(n)]
    pairs += [(2 * i + 1, 2 * ((i - by) % n) + 1) for i in range(n)]
    with jax.named_scope(tag):
        return lax.ppermute(a, (axis, "c"), pairs)


def together(*arrays):
    return lax.optimization_barrier(arrays)


def half(a, which):
    r, n = a.shape
    return lax.dynamic_index_in_dim(a.reshape(2, r // 2, n), which, 0, keepdims=False)


def place(own, got, other, n, me, d, c):
    r, cols = own.shape
    buf = jnp.zeros((2 * n, r // 2, cols), own.dtype)

    def put(buf, a, at):
        return lax.dynamic_update_slice(buf, a.reshape(-1, r // 2, cols), (at, 0, 0))

    buf = put(buf, own, 2 * me)
    for k in range(1, n // 2):
        buf = put(buf, got[k - 1], 2 * lax.rem(me - k * d + n, n))
        buf = put(buf, other[k - 1], 2 * lax.rem(me + k * d + n, n))
    far = 2 * lax.rem(me + n // 2, n)
    buf = put(buf, got[-1], far + c)
    buf = put(buf, other[-1], far + 1 - c)
    return buf.reshape(n * r, cols)


def norm_kernel(v_ref, la_ref, lb_ref):
    def step(i, _):
        rows = pl.ds(pl.multiple_of(i * 16, 16), 16)
        v = v_ref[rows, :].astype(jnp.float32)
        center = v - jnp.mean(v, axis=-1, keepdims=True)
        spread = jnp.mean(center * center, axis=-1, keepdims=True)
        out = center * lax.rsqrt(spread + 1e-06)
        for y in range(NY):
            lb_ref[y, rows, :] = out[:, y * NZ * WR:(y + 1) * NZ * WR].astype(jnp.bfloat16)
        for z in range(NZ):
            parts = [out[:, (y * NZ + z) * WR:(y * NZ + z + 1) * WR] for y in range(NY)]
            la_ref[z, rows, :] = jnp.concatenate(parts, axis=1).astype(jnp.bfloat16)
        return 0

    lax.fori_loop(0, v_ref.shape[0] // 16, step, 0)


def layer_norm(video, part):
    tm = 64
    low, rows = SPLIT[part] // tm, SPLIT[part + 1] - SPLIT[part]
    return pl.pallas_call(
        norm_kernel,
        grid=(rows // tm,),
        in_specs=[pl.BlockSpec((tm, DM), lambda i: (low + i, 0))],
        out_specs=[
            pl.BlockSpec((NZ, tm, NY * WR), lambda i: (0, i, 0)),
            pl.BlockSpec((NY, tm, NZ * WR), lambda i: (0, i, 0)),
        ],
        out_shape=[
            jax.ShapeDtypeStruct((NZ, rows, NY * WR), jnp.bfloat16),
            jax.ShapeDtypeStruct((NY, rows, NZ * WR), jnp.bfloat16),
        ],
        compiler_params=pltpu.CompilerParams(vmem_limit_bytes=32 * 1024 * 1024),
        cost_estimate=pl.CostEstimate(flops=60_000 * rows, bytes_accessed=30_000 * rows, transcendentals=0),
        name="norm",
    )(video)


def project_kernel(n, chunks, first, last, at_ref, *refs):
    l_refs, refs = refs[:PARTS], refs[PARTS:]
    q_ref = refs[-2] if last else refs[-1]
    at = 0
    rights = []
    for count in chunks:
        got = [r[...] for r in refs[at:at + count]]
        at += count
        if count == 2:
            even = at_ref[len(chunks)] == 0
            got = [jnp.where(even, got[0], got[1]), jnp.where(even, got[1], got[0])]
        per = n // count
        got = [w.reshape(per, BR, w.shape[-1])[:, :WR].reshape(per * WR, w.shape[-1]) for w in got]
        rights.append(got[0] if count == 1 else jnp.concatenate(got, axis=0))
    for h, l_ref in enumerate(l_refs):
        rows = slice(SPLIT[h], SPLIT[h + 1])
        total = None if first else refs[at][rows, :]
        for k, w in enumerate(rights):
            part = jnp.dot(l_ref[at_ref[k]], w, preferred_element_type=jnp.float32)
            total = part if total is None else total + part
        q_ref[rows, :] = total
        if last:
            square = total * total
            lanes = square[:, :128]
            for j in range(128, square.shape[1], 128):
                lanes = lanes + square[:, j:j + 128]
            refs[-1][:, rows] = jnp.sum(lanes.T, axis=0, keepdims=True)


def project(q, n, at, c, left, chunks, last=False):
    vm = pl.BlockSpec(memory_space=pltpu.VMEM)
    sm = pl.BlockSpec(memory_space=pltpu.SMEM)
    flat = [a for chunk in chunks for a in chunk]
    cols = flat[0].shape[-1]
    first = q is None
    at = jnp.stack([*at, c]).astype(jnp.int32)
    extra = [] if first else [q]
    q_shape = jax.ShapeDtypeStruct((TOK, cols), jnp.float32)
    return pl.pallas_call(
        functools.partial(project_kernel, n, [len(chunk) for chunk in chunks], first, last),
        in_specs=[sm] + [vm] * (PARTS + len(flat) + len(extra)),
        out_specs=[vm, vm] if last else vm,
        out_shape=[q_shape, jax.ShapeDtypeStruct((1, TOK), jnp.float32)] if last else q_shape,
        input_output_aliases={} if first else {1 + PARTS + len(flat): 0},
        compiler_params=pltpu.CompilerParams(vmem_limit_bytes=40 * 1024 * 1024),
        cost_estimate=pl.CostEstimate(
            flops=2 * TOK * n * WR * cols * len(chunks),
            bytes_accessed=len(chunks) * 2_000_000 + 2_600_000, transcendentals=0),
        name="project",
    )(at, *left, *flat, *extra)


def attend_kernel(len_ref, qa_ref, qb_ref, s0, s1, s2, s3, ck_ref, cv_ref, na_ref, nb_ref, o_ref, r_ref, one_ref, cm_ref, nm_ref):
    head = pl.program_id(0)

    @pl.when(head == 0)
    def _():
        squares = (s0[...] + s1[...]) + (s2[...] + s3[...])
        r = lax.rsqrt(squares * (1.0 / DM) + 1e-06)
        r_ref[...] = jnp.broadcast_to(r, (HD, TOK)).T
        lane = lax.broadcasted_iota(jnp.int32, (PLEN, HD), 1)
        slot = lax.broadcasted_iota(jnp.int32, (PLEN, HD), 0)
        one_ref[...] = jnp.where(lane == 0, 1.0, 0.0).astype(jnp.bfloat16)
        for m_ref, length in ((cm_ref, len_ref[0]), (nm_ref, len_ref[1])):
            dead = jnp.logical_and(lane == 0, slot >= length)
            m_ref[...] = jnp.where(dead, -1e30, 0.0).astype(jnp.bfloat16)

    in_a = head < NA // HD
    q = (jnp.where(in_a, qa_ref[...], qb_ref[...]) * r_ref[...]).astype(jnp.bfloat16)
    q = jnp.concatenate([q, one_ref[...]], axis=1)
    neg = jnp.where(in_a, na_ref[...], nb_ref[...])
    scale = math.log2(math.e) / math.sqrt(HD)

    def one(k, m, v):
        k = jnp.concatenate([k, m], axis=1)
        s = lax.dot_general(q, k, (((1,), (1,)), ((), ())), preferred_element_type=jnp.float32)
        e = jnp.exp2((s - jnp.max(s, axis=-1, keepdims=True)) * scale)
        w = (e * (1.0 / jnp.sum(e, axis=-1, keepdims=True))).astype(jnp.bfloat16)
        return jnp.dot(w, v, preferred_element_type=jnp.float32)

    cond = one(ck_ref[...], cm_ref[...], cv_ref[...])
    uncond = one(neg[0], nm_ref[...], neg[1])
    o_ref[...] = (uncond + GUIDE * (cond - uncond)).astype(jnp.bfloat16)


def attend(lens, qa, qb, squares, ck, cv, na, nb):
    col = pl.BlockSpec((TOK, HD), lambda h: (0, h))
    row = pl.BlockSpec((1, TOK), lambda h: (0, 0))
    last_a = NA // HD - 1
    in_a = lambda h: jnp.minimum(h, last_a)
    in_b = lambda h: jnp.maximum(h - last_a - 1, 0)
    return pl.pallas_call(
        attend_kernel,
        grid=(COLS // HD,),
        in_specs=[
            pl.BlockSpec(memory_space=pltpu.SMEM),
            pl.BlockSpec((TOK, HD), lambda h: (0, in_a(h))),
            pl.BlockSpec((TOK, HD), lambda h: (0, in_b(h))),
            row, row, row, row,
            col, col,
            pl.BlockSpec((2, PLEN, HD), lambda h: (0, 0, in_a(h))),
            pl.BlockSpec((2, PLEN, HD), lambda h: (0, 0, in_b(h))),
        ],
        out_specs=col,
        out_shape=jax.ShapeDtypeStruct((TOK, COLS), jnp.bfloat16),
        scratch_shapes=[pltpu.VMEM((TOK, HD), jnp.float32)] + [pltpu.VMEM((TOK, HD), jnp.bfloat16)] * 3,
        compiler_params=pltpu.CompilerParams(vmem_limit_bytes=32 * 1024 * 1024),
        cost_estimate=pl.CostEstimate(flops=8 * TOK * PLEN * COLS, bytes_accessed=10_000_000, transcendentals=2 * TOK * PLEN * 10),
        name="attend",
    )(lens, qa, qb, *squares, ck, cv, na, nb)


def body(video, w_query, cond_kv, neg_kv, prompt_len, neg_len):
    y, z, c = lax.axis_index("y"), lax.axis_index("z"), lax.axis_index("c")
    d = 1 - 2 * c

    neg = neg_kv.transpose(1, 0, 2).reshape(2 * NEGS, COLS)
    own = jnp.concatenate([w_query, neg], axis=0)
    oth = swap_cores(own, "s0")
    first = jnp.where(c == 0, own, oth)
    second = jnp.where(c == 0, oth, own)
    block = jnp.concatenate([first[:ROWS], second[:ROWS], first[ROWS:], second[ROWS:]], axis=0)
    a0, b0 = block[:, :NA], block[:, NA:]

    def norm(i, *deps):
        with jax.named_scope(f"norm{i}"):
            return layer_norm(together(video, *deps)[0] if deps else video, i)

    def finish(got, tag):
        both = swap_cores(jnp.concatenate(got, axis=0), tag)
        out, at = [], 0
        for g in got:
            out.append(both[at:at + g.shape[0]])
            at += g.shape[0]
        return out

    ay1 = shift(a0, "y", NY, "ay1")
    bz1 = shift(b0, "z", NZ, "bz1")
    bz2 = shift(b0, "z", NZ, "bz2", 2)
    n0 = norm(0)
    ay1, bz1, bz2, n0 = together(ay1, bz1, bz2, n0)

    ay2 = shift(half(ay1, c), "y", NY, "ay2")
    bz3 = shift(bz2, "z", NZ, "bz3")
    bz4 = shift(half(bz2, c), "z", NZ, "bz4", 2)
    a1 = place(a0, [ay1, ay2], finish([ay1, ay2], "as"), NY, y, d, c)
    a1, cond_kv = together(a1, cond_kv)
    af0, ag0 = half(a1, c), half(a1, 1 - c)
    af1 = shift(af0, "z", NZ, "af1")
    n1 = norm(1, n0[0], a1)
    bz = [bz1, bz2, bz3, bz4]
    b1 = place(b0, bz, finish(bz, "bs"), NZ, z, d, c)
    n1, ag0, b1 = together(n1, ag0, b1)
    ag1 = shift(ag0, "z", NZ, "ag1")
    bf0, bg0 = half(b1, c), half(b1, 1 - c)
    bf1, bg1 = shift(bf0, "y", NY, "bf1"), shift(bg0, "y", NY, "bg1")
    af1, n1 = together(af1, n1)
    af2 = shift(af1, "z", NZ, "af2")
    ag2 = shift(ag1, "z", NZ, "ag2")
    af2, bf1 = together(af2, bf1)
    bf2 = shift(bf1, "y", NY, "bf2")
    af3 = shift(af2, "z", NZ, "af3")
    ag3 = shift(ag2, "z", NZ, "ag3")
    af4 = shift(af3, "z", NZ, "af4")
    az = [(af1, ag1), (af2, ag2), (af3, ag3), (af4,)]
    by = [(bf1, bg1), (bf2,)]
    norms = (n0, n1)
    la, lb = [m[0] for m in norms], [m[1] for m in norms]

    def other(hop, tag):
        return tuple(swap_cores(a, tag + t) for a, t in zip(hop, "fg"))

    azo = [other(h, f"as{k}") for k, h in enumerate(az, 1)]
    byo = [other(h, f"bs{k}") for k, h in enumerate(by, 1)]

    def at(me, k, n):
        return lax.rem(me + k * d + n, n)

    qa = project(None, NY, [z], c, la, [(a1,)])
    qb = project(None, NZ, [y], c, lb, [(b1,)])
    for k in range(1, NZ // 2):
        qa = project(qa, NY, [at(z, -k, NZ), at(z, k, NZ)], c, la, [az[k - 1], azo[k - 1][::-1]])
    qa, sa = project(qa, NY, [at(z, NZ // 2, NZ)], c, la, [(az[-1][0], azo[-1][0])], last=True)
    for k in range(1, NY // 2):
        qb = project(qb, NZ, [at(y, -k, NY), at(y, k, NY)], c, lb, [by[k - 1], byo[k - 1][::-1]])
    qb, sb = project(qb, NZ, [at(y, NY // 2, NY)], c, lb, [(by[-1][0], byo[-1][0])], last=True)
    part = sa + sb
    squares = [part] + [lax.ppermute(part, "x", [(i, (i + k) % NX) for i in range(NX)]) for k in (1, 2, 3)]

    def negative(own, hops, others, n, me):
        m = 2 * len(hops)
        cols = own.shape[-1]
        buf = jnp.zeros((m, 2, n // 2, BR - WR, cols), own.dtype)

        def put(buf, a, at, which):
            rows = a.reshape(-1, n // 2, BR, cols)[:, :, WR:]
            return lax.dynamic_update_slice(buf, rows[None], (at, which, 0, 0, 0))

        buf = put(buf, own, me, 0)
        for k in range(1, m // 2):
            for i, which in enumerate((c, 1 - c)):
                buf = put(buf, hops[k - 1][i], at(me, -k, m), which)
                buf = put(buf, others[k - 1][i], at(me, k, m), 1 - which)
        far = at(me, m // 2, m)
        buf = put(buf, hops[-1][0], far, c)
        buf = put(buf, others[-1][0], far, 1 - c)
        return buf.reshape(m, n, NC, 2, NEGS, cols)

    na = negative(a1, az, azo, NY, z).transpose(3, 1, 0, 2, 4, 5).reshape(2, PLEN, NA)
    nb = negative(b1, by, byo, NZ, y).transpose(3, 0, 1, 2, 4, 5).reshape(2, PLEN, NB)
    ck, cv = cond_kv[0, :, 0], cond_kv[0, :, 1]
    lens = jnp.concatenate([prompt_len, neg_len])
    return attend(lens, qa, qb, squares, ck, cv, na, nb)


def solution(mesh):
    mesh4 = Mesh(mesh.devices.reshape(NY, NZ, NC, NX), ("y", "z", "c", "x"))
    bag = ("y", "z", "c")
    in_specs = (
        P(bag, None),
        P(bag, "x"),
        P(bag, None, None, "x"),
        P(bag, None, "x"),
        P(bag),
        P(),
    )
    return jax.shard_map(body, mesh=mesh4, in_specs=in_specs, out_specs=P(bag, "x"), check_vma=False)
```

```python
import functools
import math

import jax
import jax.numpy as jnp
from jax import lax
from jax.experimental import pallas as pl
from jax.experimental.pallas import tpu as pltpu
from jax.sharding import Mesh, PartitionSpec as P

DM = 5120
HD = 128
TOK = 512
SPLIT = (0, 128, TOK)
PARTS = len(SPLIT) - 1
PLEN = 512
NY, NZ, NC, NX = 4, 8, 2, 4
COLS = DM // NX
NA = 640
NB = COLS - NA
ROWS = DM // (NY * NZ * NC)
NEGS = PLEN // (NY * NZ * NC)
WR = NC * ROWS
BR = NC * (ROWS + 2 * NEGS)
GUIDE = 5.0
VMEM_LIMIT = 60 * 1024 * 1024


def swap_cores(a, tag):
    with jax.named_scope(tag):
        return lax.ppermute(a, "c", [(0, 1), (1, 0)])


def shift(a, axis, n, tag, by=1):
    pairs = [(2 * i, 2 * ((i + by) % n)) for i in range(n)]
    pairs += [(2 * i + 1, 2 * ((i - by) % n) + 1) for i in range(n)]
    with jax.named_scope(tag):
        return lax.ppermute(a, (axis, "c"), pairs)


def together(*arrays):
    return lax.optimization_barrier(arrays)


def half(a, which):
    r, n = a.shape
    return lax.dynamic_index_in_dim(a.reshape(2, r // 2, n), which, 0, keepdims=False)


def place(own, got, other, n, me, d, c):
    r, cols = own.shape
    buf = jnp.zeros((2 * n, r // 2, cols), own.dtype)

    def put(buf, a, at):
        return lax.dynamic_update_slice(buf, a.reshape(-1, r // 2, cols), (at, 0, 0))

    buf = put(buf, own, 2 * me)
    for k in range(1, n // 2):
        buf = put(buf, got[k - 1], 2 * lax.rem(me - k * d + n, n))
        buf = put(buf, other[k - 1], 2 * lax.rem(me + k * d + n, n))
    far = 2 * lax.rem(me + n // 2, n)
    buf = put(buf, got[-1], far + c)
    buf = put(buf, other[-1], far + 1 - c)
    return buf.reshape(n * r, cols)


def norm_kernel(v_ref, la_ref, lb_ref):
    def step(i, _):
        rows = pl.ds(pl.multiple_of(i * 16, 16), 16)
        v = v_ref[rows, :].astype(jnp.float32)
        center = v - jnp.mean(v, axis=-1, keepdims=True)
        spread = jnp.mean(center * center, axis=-1, keepdims=True)
        out = center * lax.rsqrt(spread + 1e-06)
        for y in range(NY):
            lb_ref[y, rows, :] = out[:, y * NZ * WR:(y + 1) * NZ * WR].astype(jnp.bfloat16)
        for z in range(NZ):
            parts = [out[:, (y * NZ + z) * WR:(y * NZ + z + 1) * WR] for y in range(NY)]
            la_ref[z, rows, :] = jnp.concatenate(parts, axis=1).astype(jnp.bfloat16)
        return 0

    lax.fori_loop(0, v_ref.shape[0] // 16, step, 0)


def layer_norm(video, part):
    tm = 64
    low, rows = SPLIT[part] // tm, SPLIT[part + 1] - SPLIT[part]
    return pl.pallas_call(
        norm_kernel,
        grid=(rows // tm,),
        in_specs=[pl.BlockSpec((tm, DM), lambda i: (low + i, 0))],
        out_specs=[
            pl.BlockSpec((NZ, tm, NY * WR), lambda i: (0, i, 0)),
            pl.BlockSpec((NY, tm, NZ * WR), lambda i: (0, i, 0)),
        ],
        out_shape=[
            jax.ShapeDtypeStruct((NZ, rows, NY * WR), jnp.bfloat16),
            jax.ShapeDtypeStruct((NY, rows, NZ * WR), jnp.bfloat16),
        ],
        compiler_params=pltpu.CompilerParams(vmem_limit_bytes=32 * 1024 * 1024),
        cost_estimate=pl.CostEstimate(flops=60_000 * rows, bytes_accessed=30_000 * rows, transcendentals=0),
        name="norm",
    )(video)


def project_kernel(n, chunks, first, last, at_ref, *refs):
    l_refs, refs = refs[:PARTS], refs[PARTS:]
    q_ref = refs[-2] if last else refs[-1]
    at = 0
    rights = []
    for count in chunks:
        got = [r[...] for r in refs[at:at + count]]
        at += count
        if count == 2:
            even = at_ref[len(chunks)] == 0
            got = [jnp.where(even, got[0], got[1]), jnp.where(even, got[1], got[0])]
        per = n // count
        got = [w.reshape(per, BR, w.shape[-1])[:, :WR].reshape(per * WR, w.shape[-1]) for w in got]
        rights.append(got[0] if count == 1 else jnp.concatenate(got, axis=0))
    for h, l_ref in enumerate(l_refs):
        rows = slice(SPLIT[h], SPLIT[h + 1])
        total = None if first else refs[at][rows, :]
        for k, w in enumerate(rights):
            part = jnp.dot(l_ref[at_ref[k]], w, preferred_element_type=jnp.float32)
            total = part if total is None else total + part
        q_ref[rows, :] = total
        if last:
            square = total * total
            lanes = square[:, :128]
            for j in range(128, square.shape[1], 128):
                lanes = lanes + square[:, j:j + 128]
            refs[-1][:, rows] = jnp.sum(lanes.T, axis=0, keepdims=True)


def project(q, n, at, c, left, chunks, last=False):
    vm = pl.BlockSpec(memory_space=pltpu.VMEM)
    sm = pl.BlockSpec(memory_space=pltpu.SMEM)
    flat = [a for chunk in chunks for a in chunk]
    cols = flat[0].shape[-1]
    first = q is None
    at = jnp.stack([*at, c]).astype(jnp.int32)
    extra = [] if first else [q]
    q_shape = jax.ShapeDtypeStruct((TOK, cols), jnp.float32)
    return pl.pallas_call(
        functools.partial(project_kernel, n, [len(chunk) for chunk in chunks], first, last),
        in_specs=[sm] + [vm] * (PARTS + len(flat) + len(extra)),
        out_specs=[vm, vm] if last else vm,
        out_shape=[q_shape, jax.ShapeDtypeStruct((1, TOK), jnp.float32)] if last else q_shape,
        input_output_aliases={} if first else {1 + PARTS + len(flat): 0},
        compiler_params=pltpu.CompilerParams(vmem_limit_bytes=40 * 1024 * 1024),
        cost_estimate=pl.CostEstimate(
            flops=2 * TOK * n * WR * cols * len(chunks),
            bytes_accessed=len(chunks) * 2_000_000 + 2_600_000, transcendentals=0),
        name="project",
    )(at, *left, *flat, *extra)


def attend_kernel(len_ref, qa_ref, qb_ref, s0, s1, s2, s3, ck_ref, cv_ref, na_ref, nb_ref, o_ref, r_ref, one_ref, cm_ref, nm_ref):
    head = pl.program_id(0)

    @pl.when(head == 0)
    def _():
        squares = (s0[...] + s1[...]) + (s2[...] + s3[...])
        r = lax.rsqrt(squares * (1.0 / DM) + 1e-06)
        r_ref[...] = jnp.broadcast_to(r, (HD, TOK)).T
        lane = lax.broadcasted_iota(jnp.int32, (PLEN, HD), 1)
        slot = lax.broadcasted_iota(jnp.int32, (PLEN, HD), 0)
        one_ref[...] = jnp.where(lane == 0, 1.0, 0.0).astype(jnp.bfloat16)
        for m_ref, length in ((cm_ref, len_ref[0]), (nm_ref, len_ref[1])):
            dead = jnp.logical_and(lane == 0, slot >= length)
            m_ref[...] = jnp.where(dead, -1e30, 0.0).astype(jnp.bfloat16)

    in_a = head < NA // HD
    q = (jnp.where(in_a, qa_ref[...], qb_ref[...]) * r_ref[...]).astype(jnp.bfloat16)
    q = jnp.concatenate([q, one_ref[...]], axis=1)
    neg = jnp.where(in_a, na_ref[...], nb_ref[...])
    scale = math.log2(math.e) / math.sqrt(HD)

    def one(k, m, v):
        k = jnp.concatenate([k, m], axis=1)
        s = lax.dot_general(q, k, (((1,), (1,)), ((), ())), preferred_element_type=jnp.float32)
        e = jnp.exp2((s - jnp.max(s, axis=-1, keepdims=True)) * scale)
        w = (e * (1.0 / jnp.sum(e, axis=-1, keepdims=True))).astype(jnp.bfloat16)
        return jnp.dot(w, v, preferred_element_type=jnp.float32)

    cond = one(ck_ref[...], cm_ref[...], cv_ref[...])
    uncond = one(neg[0], nm_ref[...], neg[1])
    o_ref[...] = (uncond + GUIDE * (cond - uncond)).astype(jnp.bfloat16)


def attend(lens, qa, qb, squares, ck, cv, na, nb):
    col = pl.BlockSpec((TOK, HD), lambda h: (0, h))
    row = pl.BlockSpec((1, TOK), lambda h: (0, 0))
    last_a = NA // HD - 1
    in_a = lambda h: jnp.minimum(h, last_a)
    in_b = lambda h: jnp.maximum(h - last_a - 1, 0)
    return pl.pallas_call(
        attend_kernel,
        grid=(COLS // HD,),
        in_specs=[
            pl.BlockSpec(memory_space=pltpu.SMEM),
            pl.BlockSpec((TOK, HD), lambda h: (0, in_a(h))),
            pl.BlockSpec((TOK, HD), lambda h: (0, in_b(h))),
            row, row, row, row,
            col, col,
            pl.BlockSpec((2, PLEN, HD), lambda h: (0, 0, in_a(h))),
            pl.BlockSpec((2, PLEN, HD), lambda h: (0, 0, in_b(h))),
        ],
        out_specs=col,
        out_shape=jax.ShapeDtypeStruct((TOK, COLS), jnp.bfloat16),
        scratch_shapes=[pltpu.VMEM((TOK, HD), jnp.float32)] + [pltpu.VMEM((TOK, HD), jnp.bfloat16)] * 3,
        compiler_params=pltpu.CompilerParams(vmem_limit_bytes=32 * 1024 * 1024),
        cost_estimate=pl.CostEstimate(flops=8 * TOK * PLEN * COLS, bytes_accessed=10_000_000, transcendentals=2 * TOK * PLEN * 10),
        name="attend",
    )(lens, qa, qb, *squares, ck, cv, na, nb)


def body(video, w_query, cond_kv, neg_kv, prompt_len, neg_len):
    y, z, c = lax.axis_index("y"), lax.axis_index("z"), lax.axis_index("c")
    d = 1 - 2 * c

    neg = neg_kv.transpose(1, 0, 2).reshape(2 * NEGS, COLS)
    own = jnp.concatenate([w_query, neg], axis=0)
    oth = swap_cores(own, "s0")
    first = jnp.where(c == 0, own, oth)
    second = jnp.where(c == 0, oth, own)
    block = jnp.concatenate([first[:ROWS], second[:ROWS], first[ROWS:], second[ROWS:]], axis=0)
    a0, b0 = block[:, :NA], block[:, NA:]

    def norm(i, *deps):
        with jax.named_scope(f"norm{i}"):
            return layer_norm(together(video, *deps)[0] if deps else video, i)

    def finish(got, tag):
        both = swap_cores(jnp.concatenate(got, axis=0), tag)
        out, at = [], 0
        for g in got:
            out.append(both[at:at + g.shape[0]])
            at += g.shape[0]
        return out

    ay1 = shift(a0, "y", NY, "ay1")
    bz1 = shift(b0, "z", NZ, "bz1")
    bz2 = shift(b0, "z", NZ, "bz2", 2)
    n0 = norm(0)
    bz1, bz2, n0 = together(bz1, bz2, n0)

    ay2 = shift(half(ay1, c), "y", NY, "ay2")
    bz3 = shift(bz2, "z", NZ, "bz3")
    bz4 = shift(half(bz2, c), "z", NZ, "bz4", 2)
    a1 = place(a0, [ay1, ay2], finish([ay1, ay2], "as"), NY, y, d, c)
    a1, cond_kv = together(a1, cond_kv)
    af0, ag0 = half(a1, c), half(a1, 1 - c)
    af1 = shift(af0, "z", NZ, "af1")
    n1 = norm(1, n0[0], a1)
    bz = [bz1, bz2, bz3, bz4]
    b1 = place(b0, bz, finish(bz, "bs"), NZ, z, d, c)
    n1, ag0, b1 = together(n1, ag0, b1)
    ag1 = shift(ag0, "z", NZ, "ag1")
    bf0, bg0 = half(b1, c), half(b1, 1 - c)
    bf1, bg1 = shift(bf0, "y", NY, "bf1"), shift(bg0, "y", NY, "bg1")
    af1, n1 = together(af1, n1)
    af2 = shift(af1, "z", NZ, "af2")
    ag2 = shift(ag1, "z", NZ, "ag2")
    af2, bf1 = together(af2, bf1)
    bf2 = shift(bf1, "y", NY, "bf2")
    af3 = shift(af2, "z", NZ, "af3")
    ag3 = shift(ag2, "z", NZ, "ag3")
    af4 = shift(af3, "z", NZ, "af4")
    az = [(af1, ag1), (af2, ag2), (af3, ag3), (af4,)]
    by = [(bf1, bg1), (bf2,)]
    norms = (n0, n1)
    la, lb = [m[0] for m in norms], [m[1] for m in norms]

    def other(hop, tag):
        return tuple(swap_cores(a, tag + t) for a, t in zip(hop, "fg"))

    azo = [other(h, f"as{k}") for k, h in enumerate(az, 1)]
    byo = [other(h, f"bs{k}") for k, h in enumerate(by, 1)]

    def at(me, k, n):
        return lax.rem(me + k * d + n, n)

    qa = project(None, NY, [z], c, la, [(a1,)])
    qb = project(None, NZ, [y], c, lb, [(b1,)])
    for k in range(1, NZ // 2):
        qa = project(qa, NY, [at(z, -k, NZ), at(z, k, NZ)], c, la, [az[k - 1], azo[k - 1][::-1]])
    qa, sa = project(qa, NY, [at(z, NZ // 2, NZ)], c, la, [(az[-1][0], azo[-1][0])], last=True)
    for k in range(1, NY // 2):
        qb = project(qb, NZ, [at(y, -k, NY), at(y, k, NY)], c, lb, [by[k - 1], byo[k - 1][::-1]])
    qb, sb = project(qb, NZ, [at(y, NY // 2, NY)], c, lb, [(by[-1][0], byo[-1][0])], last=True)
    part = sa + sb
    squares = [part] + [lax.ppermute(part, "x", [(i, (i + k) % NX) for i in range(NX)]) for k in (1, 2, 3)]

    def negative(own, hops, others, n, me):
        m = 2 * len(hops)
        cols = own.shape[-1]
        buf = jnp.zeros((m, 2, n // 2, BR - WR, cols), own.dtype)

        def put(buf, a, at, which):
            rows = a.reshape(-1, n // 2, BR, cols)[:, :, WR:]
            return lax.dynamic_update_slice(buf, rows[None], (at, which, 0, 0, 0))

        buf = put(buf, own, me, 0)
        for k in range(1, m // 2):
            for i, which in enumerate((c, 1 - c)):
                buf = put(buf, hops[k - 1][i], at(me, -k, m), which)
                buf = put(buf, others[k - 1][i], at(me, k, m), 1 - which)
        far = at(me, m // 2, m)
        buf = put(buf, hops[-1][0], far, c)
        buf = put(buf, others[-1][0], far, 1 - c)
        return buf.reshape(m, n, NC, 2, NEGS, cols)

    na = negative(a1, az, azo, NY, z).transpose(3, 1, 0, 2, 4, 5).reshape(2, PLEN, NA)
    nb = negative(b1, by, byo, NZ, y).transpose(3, 0, 1, 2, 4, 5).reshape(2, PLEN, NB)
    ck, cv = cond_kv[0, :, 0], cond_kv[0, :, 1]
    lens = jnp.concatenate([prompt_len, neg_len])
    return attend(lens, qa, qb, squares, ck, cv, na, nb)


def solution(mesh):
    mesh4 = Mesh(mesh.devices.reshape(NY, NZ, NC, NX), ("y", "z", "c", "x"))
    bag = ("y", "z", "c")
    in_specs = (
        P(bag, None),
        P(bag, "x"),
        P(bag, None, None, "x"),
        P(bag, None, "x"),
        P(bag),
        P(),
    )
    return jax.shard_map(body, mesh=mesh4, in_specs=in_specs, out_specs=P(bag, "x"), check_vma=False)
```
